32 devices in a mesh: rows: 8 (over z, x), probe: 4 (over y, core).
Axes of the slice: x: 2, y: 2, z: 4, core: 2. Of those that a mesh axis runs over, the one named last changes fastest.
Arguments:
- start_block: float32 [8, 32768], P('probe', 'rows'), may hold values from -6 to 6
- blocks: bfloat16 [1024, 128, 128], P('rows'), may hold values from 0 to 3, as said below
- block_rows: int32 [1024], P('rows'), may hold values from 0 to 31
- block_cols: int32 [1024], P('rows'), may hold values from 0 to 63
- counts: int32 [8], P('rows'), may hold values from 32 to 128, as said below
- boundary: int32 [2, 16384], P(None, 'rows'), may hold values from 0 to 4095, as said below
Outputs:
- basis: float32 [8, 32768], P('probe', 'rows')
- alpha_blocks: float32 [3, 8, 8], replicated
- beta_blocks: float32 [3, 8, 8], replicated
The draws below stay inside these ranges and needn't reach their ends.
Inputs may be any that keep to these rules, and one draw needn't show every extreme that they name: `blocks`: nonnegative edge weights, most entries zero. `counts`: one or more partitions have all 128 slots live. `boundary`: the 2048 entries of one list for one partition are distinct rows of that partition.
All inputs are finite; a program needn't handle non-finite values.
Results may differ from the reference program's by a relative error of at most 0.00525.
Values may be sent and summed in bfloat16 or wider, within the bound.
A program may use at most 64 MiB of HBM per device.

```python
import jax
import jax.numpy as jnp
from jax import lax

PROBES = 8
BLOCK = 128
ROW_BLOCKS = 32
STEPS = 3
HALO = 2048
MAXB = 128
NODES = 32768
N_ROWS = 8


def draw_blocks(key, part):
    shape = (N_ROWS * MAXB, BLOCK, BLOCK)
    pick_key, value_key = jax.random.split(key)
    chance = jax.random.uniform(pick_key, shape, jnp.float32)
    weight = jnp.exp(jax.random.uniform(value_key, shape, jnp.float32, jnp.log(0.2), jnp.log(2.0)))
    return jnp.where(chance < 0.15, weight, 0.0).astype(jnp.bfloat16)


def draw_counts(key, part):
    first_key, second_key = jax.random.split(key)
    divisor = jax.random.randint(first_key, (N_ROWS,), 1, 5)
    live_slots = MAXB // divisor
    chosen = jax.random.randint(second_key, (), 0, N_ROWS)
    return jnp.where(jnp.arange(N_ROWS) == chosen, MAXB, live_slots).astype(jnp.int32)


def draw_boundary(key, part):
    keys_all = jax.random.split(key, 2 * N_ROWS)
    rows_dev = ROW_BLOCKS * BLOCK
    orders = jax.vmap(lambda one_key: jax.random.permutation(one_key, rows_dev))(keys_all)
    return orders[:, :HALO].reshape(2, N_ROWS * HALO).astype(jnp.int32)


def touch_ends(entries, own_key, smallest, top_value):
    longest = entries.shape.index(max(entries.shape))
    spots = []
    for shift in (0, 1):
        where = [jax.random.randint(jax.random.fold_in(own_key, axis), (), 0, length) for axis, length in enumerate(entries.shape)]
        where[longest] = (where[longest] + shift) % entries.shape[longest]
        spots.append(tuple(where))
    return entries.at[spots[0]].set(smallest).at[spots[1]].set(top_value)


def block_scale(rng, shape, pieces, low, high):
    factor_of = 1.0
    for position, parts in pieces:
        heights = jax.random.uniform(jax.random.fold_in(jax.random.fold_in(rng, 6), position), (parts,), jnp.float32, low / len(pieces), high / len(pieces))
        factor_of = factor_of * jnp.repeat(jnp.exp(heights), shape[position] // parts).reshape((-1,) + (1,) * (len(shape) - 1 - position))
    return factor_of


def normal_values(rng, dims, deviation, most, shards=(), held_as=jnp.bfloat16):
    array = deviation * jax.random.normal(rng, dims, jnp.float32)
    if shards:
        array = array * block_scale(rng, dims, shards, -0.22, 0.18)
    return jnp.clip(array, -most, most).astype(held_as)


def setup_inputs(seed: int = 0) -> dict:
    arg_keys = jax.random.split(jax.random.key(seed), 7)
    return {
        "start_block": normal_values(arg_keys[0], (PROBES, NODES), 1.0, 6.0, ((0, 4), (1, 8)), jnp.float32),
        "blocks": draw_blocks(jax.random.fold_in(arg_keys[6], 71), 0),
        "block_rows": touch_ends(jax.random.randint(arg_keys[2], (N_ROWS * MAXB,), 0, ROW_BLOCKS), jax.random.fold_in(arg_keys[2], 1), 0, ROW_BLOCKS - 1).astype(jnp.int32),
        "block_cols": touch_ends(jax.random.randint(arg_keys[3], (N_ROWS * MAXB,), 0, 2 * ROW_BLOCKS), jax.random.fold_in(arg_keys[3], 1), 0, (2 * ROW_BLOCKS) - 1).astype(jnp.int32),
        "counts": draw_counts(jax.random.fold_in(arg_keys[6], 71), 0),
        "boundary": draw_boundary(jax.random.fold_in(arg_keys[6], 71), 0),
    }


def apply_graph(scaled, blocks, block_rows, block_cols, counts, boundary):
    probe_count = scaled.shape[0]
    rows_dev = ROW_BLOCKS * BLOCK
    split_rows = scaled.reshape(probe_count, N_ROWS, rows_dev)
    bound = boundary.reshape(2, N_ROWS, HALO)
    from_lower = jnp.take_along_axis(jnp.roll(split_rows, 1, axis=1), jnp.roll(bound[1], 1, axis=0)[None], axis=2)
    from_upper = jnp.take_along_axis(jnp.roll(split_rows, -1, axis=1), jnp.roll(bound[0], -1, axis=0)[None], axis=2)
    extended = jnp.concatenate([split_rows, from_lower, from_upper], axis=2)
    extended = jnp.transpose(extended, (1, 0, 2))

    def partition(inputs):
        ext_part, tiles, tile_rows, tile_cols, live_count = inputs
        is_live = (jnp.arange(MAXB, dtype=jnp.int32) < live_count).astype(jnp.float32)
        tiles32 = tiles.astype(jnp.float32)
        columns = ext_part.reshape(probe_count, 2 * ROW_BLOCKS, BLOCK)
        x_cols = columns[:, tile_cols].astype(jnp.float32)
        x_rows = columns[:, :ROW_BLOCKS][:, tile_rows].astype(jnp.float32)
        forward = jnp.einsum('pkj,kij->pki', x_cols, tiles32) * is_live[None, :, None]
        backward = jnp.einsum('pki,kij->pkj', x_rows, tiles32) * is_live[None, :, None]
        row_sums = jnp.zeros((probe_count, ROW_BLOCKS, BLOCK), jnp.float32).at[:, tile_rows].add(forward)
        col_sums = jnp.zeros((probe_count, 2 * ROW_BLOCKS, BLOCK), jnp.float32).at[:, tile_cols].add(backward)
        summed = col_sums.reshape(probe_count, 2 * rows_dev)
        return summed.at[:, :rows_dev].add(row_sums.reshape(probe_count, rows_dev))
    summed = lax.map(partition, (extended, blocks.reshape(N_ROWS, MAXB, BLOCK, BLOCK), block_rows.reshape(N_ROWS, MAXB), block_cols.reshape(N_ROWS, MAXB), counts))
    own_part = summed[:, :, :rows_dev]
    lower_part = jnp.roll(summed[:, :, rows_dev:rows_dev + HALO], -1, axis=0)
    upper_part = jnp.roll(summed[:, :, rows_dev + HALO:], 1, axis=0)
    offsets = (jnp.arange(N_ROWS, dtype=jnp.int32) * rows_dev)[:, None]
    result = jnp.transpose(own_part, (1, 0, 2)).reshape(probe_count, NODES)
    result = result.at[:, (offsets + bound[1]).reshape(-1)].add(jnp.transpose(lower_part, (1, 0, 2)).reshape(probe_count, -1))
    result = result.at[:, (offsets + bound[0]).reshape(-1)].add(jnp.transpose(upper_part, (1, 0, 2)).reshape(probe_count, -1))
    return result

def gram_mean(left, right):
    return jnp.dot(left, right.T, precision=lax.Precision.HIGHEST) / NODES

def reference(start_block, blocks, block_rows, block_cols, counts, boundary):
    unit_rows = jnp.ones((1, NODES), jnp.bfloat16)
    degree = 1.0 + apply_graph(unit_rows, blocks, block_rows, block_cols, counts, boundary)[0]
    inv_root = 1.0 / jnp.sqrt(degree)

    def laplacian(vectors):
        scaled = (inv_root * vectors).astype(jnp.bfloat16)
        image = apply_graph(scaled, blocks, block_rows, block_cols, counts, boundary)
        return vectors - inv_root * (inv_root * vectors) - inv_root * image
    factor = jnp.linalg.cholesky(gram_mean(start_block, start_block))
    current = jax.scipy.linalg.solve_triangular(factor, start_block, lower=True)
    previous = jnp.zeros_like(current)
    coupling = jnp.zeros((PROBES, PROBES), jnp.float32)
    alpha_list = []
    beta_list = []
    for iteration in range(STEPS):
        image = laplacian(current)
        alpha_block = gram_mean(image, current)
        residual = image - jnp.dot(alpha_block, current, precision=lax.Precision.HIGHEST) - jnp.dot(coupling, previous, precision=lax.Precision.HIGHEST)
        factor = jnp.linalg.cholesky(gram_mean(residual, residual))
        previous = current
        current = jax.scipy.linalg.solve_triangular(factor, residual, lower=True)
        coupling = factor.T
        alpha_list.append(alpha_block)
        beta_list.append(factor)
    return (current, jnp.stack(alpha_list), jnp.stack(beta_list))
```

```python
import functools

import jax
import jax.numpy as jnp
from jax import lax
from jax.experimental import pallas as pl
from jax.experimental.pallas import tpu as pltpu
from jax.sharding import PartitionSpec as P

STEPS = 3
LANES = 128
UNROLL = 16
MESH = pl.DeviceIdType.MESH


def kernel(
    n_rows, n_probe, node_total,
    start_ref, tiles_hbm, perm_r, keep_r, end_r, perm_c, keep_c, end_c, rows_ref, cols_ref, bound_ref, inverse_ref,
    basis_ref, alpha_ref, beta_ref,
    tiles, gathered, current, previous, image, inv_root, scaled, own, extended, halo_send, ret_send, ret_recv,
    row_sums, col_sums, gram_send, gram_recv,
    tile_sem, start_send, start_recv, halo_ssem, halo_rsem, ret_ssem, ret_rsem, gram_ssem, gram_rsem,
):
    me = lax.axis_index("rows")
    my_probe = lax.axis_index("probe")
    slots = tiles.shape[0]
    nb = current.shape[0] // 8
    nh = nb // 2
    probes_dev = start_ref.shape[0]
    lower = lax.rem(me + n_rows - 1, n_rows)
    upper = lax.rem(me + 1, n_rows)

    tile_copy = pltpu.make_async_copy(tiles_hbm, tiles, tile_sem)
    tile_copy.start()

    barrier = pltpu.get_barrier_semaphore()
    for off in range(1, n_probe):
        peer = lax.rem(my_probe + off, n_probe)
        pl.semaphore_signal(barrier, inc=1, device_id={"probe": peer}, device_id_type=MESH)

    def greet(off, carry):
        peer = lax.rem(me + off, n_rows)
        pl.semaphore_signal(barrier, inc=1, device_id={"rows": peer}, device_id_type=MESH)
        return carry

    lax.fori_loop(1, n_rows, greet, 0)
    pl.semaphore_wait(barrier, n_probe - 1 + n_rows - 1)

    def start_copy(off):
        peer = lax.rem(my_probe + off, n_probe)
        return pltpu.make_async_remote_copy(
            src_ref=start_ref,
            dst_ref=gathered.at[pl.ds(my_probe * probes_dev, probes_dev)],
            send_sem=start_send.at[off],
            recv_sem=start_recv.at[off],
            device_id={"probe": peer},
            device_id_type=MESH,
        )

    for off in range(1, n_probe):
        start_copy(off).start()
    gathered[pl.ds(my_probe * probes_dev, probes_dev)] = start_ref[...]

    def row_of(ref, block, probe):
        return jnp.broadcast_to(ref[pl.ds(block * 8 + probe, 1), :], (8, LANES))

    def block_of(ref, block):
        return ref[pl.ds(pl.multiple_of(block * 8, 8), 8), :]

    def put_block(ref, block, value):
        ref[pl.ds(pl.multiple_of(block * 8, 8), 8), :] = value

    lane = lax.broadcasted_iota(jnp.int32, (8, LANES), 1)
    sub = lax.broadcasted_iota(jnp.int32, (8, LANES), 0)
    zero = jnp.zeros((8, LANES), jnp.float32)

    def fold(accs):
        gram = zero
        for q in range(8):
            gram = jnp.where(lane == q, jnp.sum(accs[q], axis=1, keepdims=True), gram)
        return gram

    def gram_copy(index, off):
        peer = lax.rem(me + off, n_rows)
        return pltpu.make_async_remote_copy(
            src_ref=gram_send.at[index],
            dst_ref=gram_recv.at[index, me],
            send_sem=gram_ssem.at[index, off],
            recv_sem=gram_rsem.at[index, off],
            device_id={"rows": peer},
            device_id_type=MESH,
        )

    def gram_begin(index, gram):
        gram_send[index] = gram
        gram_recv[index, me] = gram

        def send(off, carry):
            gram_copy(index, off).start()
            return carry

        lax.fori_loop(1, n_rows, send, 0)

    def gram_end(index):
        def wait(off, carry):
            gram_copy(index, off).wait()
            return carry

        lax.fori_loop(1, n_rows, wait, 0)
        return jnp.sum(gram_recv[index], axis=0) * (1.0 / node_total)

    def factorise(gram):
        work = jnp.where(lane < 8, gram, jnp.where(lane == sub + 8, 1.0, 0.0))
        factor = zero
        scale = zero
        for j in range(8):
            column = jnp.broadcast_to(work[:, j : j + 1], (8, LANES))
            row = jnp.broadcast_to(work[j : j + 1, :], (8, LANES))
            pivot = jnp.broadcast_to(row[:, j : j + 1], (8, LANES))
            root = jnp.sqrt(pivot)
            factor = jnp.where((lane == j) & (sub >= j), column / root, factor)
            scale = jnp.where(sub == j, 1.0 / root, scale)
            work = work - jnp.where(sub > j, column / pivot, 0.0) * row
        work = work * scale
        return factor, work

    def columns_of(matrix, first):
        return [jnp.broadcast_to(matrix[:, first + q : first + q + 1], (8, LANES)) for q in range(8)]

    def col_products(lhs_of):
        def body(turn, acc):
            ys = []
            for u in range(UNROLL):
                m = turn * UNROLL + u
                t = perm_c[m]
                ys.append(jnp.dot(lhs_of(rows_ref, t), tiles[t], preferred_element_type=jnp.float32))
            for u in range(UNROLL):
                m = turn * UNROLL + u
                acc = acc * keep_c[m] + ys[u]
                col_sums[m] = acc
            return acc

        lax.fori_loop(0, slots // UNROLL, body, zero)

    def row_products(lhs_of):
        def body(turn, acc):
            ys = []
            for u in range(UNROLL):
                m = turn * UNROLL + u
                t = perm_r[m]
                ys.append(
                    lax.dot_general(
                        lhs_of(cols_ref, t), tiles[t], (((1,), (1,)), ((), ())), preferred_element_type=jnp.float32
                    )
                )
            for u in range(UNROLL):
                m = turn * UNROLL + u
                acc = acc * keep_r[m] + ys[u]
                row_sums[m] = acc
            return acc

        lax.fori_loop(0, slots // UNROLL, body, zero)

    def ret_copies(index):
        return [
            pltpu.make_async_remote_copy(
                src_ref=ret_send.at[index, side],
                dst_ref=ret_recv.at[index, 1 - side],
                send_sem=ret_ssem.at[index, side],
                recv_sem=ret_rsem.at[index, side],
                device_id={"rows": lower if side == 0 else upper},
                device_id_type=MESH,
            )
            for side in range(2)
        ]

    def halo_copies(index):
        return [
            pltpu.make_async_remote_copy(
                src_ref=halo_send.at[index, side],
                dst_ref=extended.at[index, pl.ds(nb + (1 - side) * nh, nh)],
                send_sem=halo_ssem.at[index, side],
                recv_sem=halo_rsem.at[index, side],
                device_id={"rows": lower if side == 0 else upper},
                device_id_type=MESH,
            )
            for side in range(2)
        ]

    def send_returns(index):
        def body(c, carry):
            for side in range(2):
                ret_send[index, side, c] = col_sums[end_c[nb + side * nh + c]]
            return carry

        lax.fori_loop(0, nh, body, 0)
        for copy in ret_copies(index):
            copy.start()

    def summed(index, block):
        total = row_sums[end_r[block]] + col_sums[end_c[block]]
        for side in range(2):
            where = jnp.broadcast_to(inverse_ref[pl.ds(side * nb + block, 1), :], (8, LANES))
            spot = jnp.bitwise_and(where, LANES - 1)
            source = jnp.right_shift(where, 7)
            found = zero
            for s in range(nh):
                picked = jnp.take_along_axis(ret_recv[index, side, s], spot, axis=1, mode="promise_in_bounds")
                found = jnp.where(source == s, picked, found)
            total = total + found
        return total

    row_sums[slots] = zero
    col_sums[slots] = zero

    for off in range(1, n_probe):
        start_copy(off).wait()

    def take_start(block, accs):
        value = jnp.stack([gathered[p, pl.ds(block, 1), :] for p in range(8)], axis=0).reshape(8, LANES)
        put_block(image, block, value)
        return accs

    lax.fori_loop(0, nb, take_start, 0)

    def gram_of(left, right):
        def body(block, accs):
            value = block_of(left, block)
            return tuple(accs[q] + value * row_of(right, block, q) for q in range(8))

        return fold(lax.fori_loop(0, nb, body, (zero,) * 8, unroll=2))

    gram_begin(0, gram_of(image, image))

    tile_copy.wait()
    ones = jnp.ones((8, LANES), jnp.bfloat16)
    col_products(lambda ref, t: ones)
    send_returns(0)
    row_products(lambda ref, t: ones)
    for copy in ret_copies(0):
        copy.wait()

    def degree_block(block, carry):
        put_block(inv_root, block, 1.0 / jnp.sqrt(1.0 + summed(0, block)))
        return carry

    lax.fori_loop(0, nb, degree_block, 0)

    factor, work = factorise(gram_end(0))

    def next_block(work, source, target):
        inverse = columns_of(work, 8)

        def body(block, carry):
            value = zero
            for q in range(8):
                value = value + inverse[q] * row_of(source, block, q)
            put_block(target, block, value)
            return carry

        lax.fori_loop(0, nb, body, 0, unroll=2)

    basis = [current, previous]
    next_block(work, image, basis[0])
    coupling = None
    for step in range(STEPS):
        now, before = basis[step % 2], basis[(step + 1) % 2]

        def scale_block(block, carry):
            value = block_of(inv_root, block) * block_of(now, block)
            put_block(scaled, block, value)
            own[block] = value.astype(jnp.bfloat16)
            extended[step, block] = value.astype(jnp.bfloat16)
            return carry

        lax.fori_loop(0, nb, scale_block, 0, unroll=4)

        def gather_block(c, carry):
            for side in range(2):
                where = jnp.broadcast_to(bound_ref[pl.ds(side * nh + c, 1), :], (8, LANES))
                spot = jnp.bitwise_and(where, LANES - 1)
                source = jnp.right_shift(where, 7)
                found = zero
                for s in range(nb):
                    picked = jnp.take_along_axis(
                        scaled[s * 8 : s * 8 + 8, :], spot, axis=1, mode="promise_in_bounds"
                    )
                    found = jnp.where(source == s, picked, found)
                halo_send[step, side, c] = found.astype(jnp.bfloat16)
            return carry

        lax.fori_loop(0, nh, gather_block, 0)
        for copy in halo_copies(step):
            copy.start()
        col_products(lambda ref, t: own[ref[t]])
        send_returns(step + 1)
        for copy in halo_copies(step):
            copy.wait()
        row_products(lambda ref, t: extended[step, ref[t]])
        for copy in ret_copies(step + 1):
            copy.wait()

        def image_block(block, accs):
            root = block_of(inv_root, block)
            value = block_of(now, block)
            value = value - root * (root * value) - root * summed(step + 1, block)
            put_block(image, block, value)
            return tuple(accs[q] + value * row_of(now, block, q) for q in range(8))

        accs = lax.fori_loop(0, nb, image_block, (zero,) * 8)
        gram_begin(1 + 2 * step, fold(accs))
        alpha = gram_end(1 + 2 * step)
        alpha_ref[step] = alpha
        alpha_cols = columns_of(alpha, 0)
        coupling_cols = columns_of(coupling, 0) if step else None

        def residual_block(block, carry):
            value = block_of(image, block)
            for q in range(8):
                value = value - alpha_cols[q] * row_of(now, block, q)
            if step:
                for q in range(8):
                    value = value - coupling_cols[q] * row_of(before, block, q)
            put_block(image, block, value)
            return carry

        lax.fori_loop(0, nb, residual_block, 0, unroll=2)
        gram_begin(2 + 2 * step, gram_of(image, image))
        factor, work = factorise(gram_end(2 + 2 * step))
        beta_ref[step] = factor
        coupling = work
        next_block(work, image, before)

    last = basis[STEPS % 2]
    for p in range(probes_dev):
        for b in range(nb):
            basis_ref[p, pl.ds(b, 1), :] = last[pl.ds(b * 8 + my_probe * probes_dev + p, 1), :]


def order_of(keys, kinds, slots):
    index = jnp.arange(slots, dtype=jnp.int32)
    unique = keys * slots + index
    rank = jnp.sum((unique[None, :] < unique[:, None]).astype(jnp.int32), axis=1)
    placed = rank[:, None] == index[None, :]
    perm = jnp.sum(jnp.where(placed, index[:, None], 0), axis=0)
    sorted_keys = jnp.sum(jnp.where(placed, keys[:, None], 0), axis=0)
    keep = jnp.concatenate([jnp.zeros((1,), jnp.bool_), sorted_keys[1:] == sorted_keys[:-1]]).astype(jnp.float32)
    kind = jnp.arange(kinds, dtype=jnp.int32)
    up_to = jnp.sum((keys[None, :] <= kind[:, None]).astype(jnp.int32), axis=1)
    some = jnp.sum((keys[None, :] == kind[:, None]).astype(jnp.int32), axis=1)
    return perm, keep, jnp.where(some > 0, up_to - 1, slots)


def inverse_of(bound, nb):
    halo = bound.shape[1]
    h = jnp.arange(halo, dtype=jnp.int32)
    in_block = jnp.right_shift(bound, 7)[:, None, :] == jnp.arange(nb, dtype=jnp.int32)[None, :, None]
    at_lane = jnp.bitwise_and(bound, LANES - 1)[:, :, None] == jnp.arange(LANES, dtype=jnp.int32)[None, None, :]
    high = jnp.where(in_block, (jnp.right_shift(h, 6) + 1)[None, None, :], 0).astype(jnp.bfloat16)
    low = jnp.where(in_block, jnp.bitwise_and(h, 63)[None, None, :], 0).astype(jnp.bfloat16)
    both = jnp.einsum(
        "lbh,lhj->lbj", jnp.concatenate([high, low], axis=1), at_lane.astype(jnp.bfloat16),
        preferred_element_type=jnp.float32,
    ).astype(jnp.int32)
    return ((both[:, :nb] - 1) * 64 + both[:, nb:]).reshape(2 * nb, LANES)


def local(start_block, blocks, block_rows, block_cols, counts, boundary):
    n_rows, n_probe = lax.axis_size("rows"), lax.axis_size("probe")
    probes_dev, rows_dev = start_block.shape
    slots = blocks.shape[0]
    nb = rows_dev // LANES
    nh = nb // 2
    live = jnp.arange(slots, dtype=jnp.int32) < counts[0]
    perm_r, keep_r, end_r = order_of(jnp.where(live, block_rows, 2 * nb), nb, slots)
    perm_c, keep_c, end_c = order_of(jnp.where(live, block_cols, 2 * nb), 2 * nb, slots)
    inverse = inverse_of(boundary, nb)
    f32, bf16 = jnp.float32, jnp.bfloat16
    n_gram = 1 + 2 * STEPS
    vmem = pl.BlockSpec(memory_space=pltpu.VMEM)
    smem = pl.BlockSpec(memory_space=pltpu.SMEM)
    dma = pltpu.SemaphoreType.DMA
    basis, alpha, beta = pl.pallas_call(
        functools.partial(kernel, n_rows, n_probe, rows_dev * n_rows),
        out_shape=(
            jax.ShapeDtypeStruct((probes_dev, nb, LANES), f32),
            jax.ShapeDtypeStruct((STEPS, 8, LANES), f32),
            jax.ShapeDtypeStruct((STEPS, 8, LANES), f32),
        ),
        in_specs=[vmem, pl.BlockSpec(memory_space=pl.ANY)] + [smem] * 8 + [vmem, vmem],
        out_specs=(vmem, vmem, vmem),
        scratch_shapes=[
            pltpu.VMEM(blocks.shape, bf16),
            pltpu.VMEM((8, nb, LANES), f32),
            pltpu.VMEM((nb * 8, LANES), f32),
            pltpu.VMEM((nb * 8, LANES), f32),
            pltpu.VMEM((nb * 8, LANES), f32),
            pltpu.VMEM((nb * 8, LANES), f32),
            pltpu.VMEM((nb * 8, LANES), f32),
            pltpu.VMEM((nb, 8, LANES), bf16),
            pltpu.VMEM((STEPS, 2 * nb, 8, LANES), bf16),
            pltpu.VMEM((STEPS, 2, nh, 8, LANES), bf16),
            pltpu.VMEM((STEPS + 1, 2, nh, 8, LANES), f32),
            pltpu.VMEM((STEPS + 1, 2, nh, 8, LANES), f32),
            pltpu.VMEM((slots + 1, 8, LANES), f32),
            pltpu.VMEM((slots + 1, 8, LANES), f32),
            pltpu.VMEM((n_gram, 8, LANES), f32),
            pltpu.VMEM((n_gram, n_rows, 8, LANES), f32),
            dma,
            dma((n_probe,)),
            dma((n_probe,)),
            dma((STEPS, 2)),
            dma((STEPS, 2)),
            dma((STEPS + 1, 2)),
            dma((STEPS + 1, 2)),
            dma((n_gram, n_rows)),
            dma((n_gram, n_rows)),
        ],
        compiler_params=pltpu.CompilerParams(
            collective_id=0, has_side_effects=True, vmem_limit_bytes=48 * 1024 * 1024
        ),
        name="lanczos",
    )(
        start_block.reshape(probes_dev, nb, LANES), blocks, perm_r, keep_r, end_r, perm_c, keep_c, end_c,
        block_rows, block_cols, boundary.reshape(2 * nh, LANES), inverse,
    )
    return basis.reshape(probes_dev, rows_dev), alpha[:, :, :8], beta[:, :, :8]


def solution(mesh):
    in_specs = (
        P("probe", "rows"),
        P("rows", None, None),
        P("rows"),
        P("rows"),
        P("rows"),
        P(None, "rows"),
    )
    out_specs = (P("probe", "rows"), P(), P())
    return jax.shard_map(local, mesh=mesh, in_specs=in_specs, out_specs=out_specs, check_vma=False)
```
